32 devices in a mesh: walk: 8 (over z, x), vec: 4 (over y, core).
Axes of the slice: x: 2, y: 2, z: 4, core: 2. Of those that a mesh axis runs over, the one named last changes fastest.
Arguments:
- walkers: bfloat16 [16, 2432, 768], P('walk')
- chol: bfloat16 [4, 8, 384, 4096], P('vec', 'walk'), may hold values from -6 to 6
- owners: int32 [4, 2], P('vec'), may hold values from 0 to 7
- branch_src: int32 [16], P('walk'), may hold values from 0 to 15, as said below
Outputs:
- branched: bfloat16 [16, 2432, 768], P('walk')
- force_bias: float32 [16, 8, 2], P('walk', 'vec')
- exchange: float32 [16, 2], P('walk')
The draws below stay inside these ranges and needn't reach their ends.
Inputs may be any that keep to these rules, and one draw needn't show every extreme that they name: `branch_src`: slot s takes its walker from the 2 walkers of block s // 2, or of the block before or after it (blocks taken cyclically).
All inputs are finite; a program needn't handle non-finite values.
Results may differ from the reference program's by a relative error of at most 0.0052.
Values may be sent and summed in bfloat16 or wider, within the bound.
A program may use at most 192 MiB of HBM per device.

```python
import jax
import jax.numpy as jnp
from jax import lax

NORB = 2048
NE = 384
W_DEV = 2
G_USE = 2
WALKERS = 16
N_WALK = 8
N_VEC = 4


def draw_walkers(key, part):
    first, second = jax.random.split(key)
    orbital = jax.random.normal(first, (WALKERS, NORB, 2 * NE), jnp.float32)
    inverse = jax.random.normal(second, (WALKERS, NE, 2 * NE), jnp.float32)
    orbital = orbital * NORB ** (-0.5)
    inverse = inverse * (0.5 / NE)
    return jnp.concatenate([orbital, inverse], axis=1).astype(jnp.bfloat16)


def draw_branch_src(key, part):
    first, second = jax.random.split(key)
    slots = jnp.arange(WALKERS, dtype=jnp.int32)
    blocks = slots // W_DEV
    offset = jax.random.randint(first, (WALKERS,), -1, 2, dtype=jnp.int32)
    within = jax.random.randint(second, (WALKERS,), 0, W_DEV, dtype=jnp.int32)
    count = WALKERS // W_DEV
    return ((blocks + offset + count) % count * W_DEV + within).astype(jnp.int32)


def set_ends(values, own_key, low, high):
    index_at = [jax.random.randint(jax.random.fold_in(own_key, axis), (), 0, length) for axis, length in enumerate(values.shape)]
    widest = values.shape.index(max(values.shape))
    beside = index_at[:widest] + [(index_at[widest] + 1) % values.shape[widest]] + index_at[widest + 1:]
    return values.at[tuple(index_at)].set(low).at[tuple(beside)].set(high)


def steps_of(rng, shape, cuts, least, high):
    gain, own = 1.0, jax.random.fold_in(rng, 6)
    for position, blocks in cuts:
        draws = jnp.exp(jax.random.uniform(jax.random.fold_in(own, position), (blocks,), jnp.float32, least / len(cuts), high / len(cuts)))
        gain = gain * jnp.repeat(draws, shape[position] // blocks).reshape([-1 if axis == position else 1 for axis in range(len(shape))])
    return gain


def normal_values(stream_key, dims, scale, bound, shards=(), held_as=jnp.bfloat16):
    entries = jax.random.normal(stream_key, dims, jnp.float32) * scale
    if len(shards) > 0:
        entries = steps_of(stream_key, dims, shards, -0.22, 0.18) * entries
    return jnp.clip(entries, min=-bound, max=bound).astype(held_as)


def setup_inputs(seed: int = 0) -> dict:
    arg_keys = jax.random.split(jax.random.key(seed), 5)
    return {
        "walkers": draw_walkers(jax.random.fold_in(arg_keys[4], 71), 0),
        "chol": normal_values(arg_keys[1], (N_VEC, N_WALK, NE, 2 * NORB), 1.0, 6.0, ((0, 4), (1, 8))),
        "owners": set_ends(jax.random.randint(arg_keys[2], (N_VEC, G_USE), 0, N_WALK), jax.random.fold_in(arg_keys[2], 1), 0, N_WALK - 1).astype(jnp.int32),
        "branch_src": draw_branch_src(jax.random.fold_in(arg_keys[4], 71), 0),
    }


def complex_block(part):
    half = part.shape[1] // 2
    lower = jnp.concatenate([-part[:, half:], part[:, :half]], axis=1)
    return jnp.concatenate([part, lower], axis=0)


def reference(walkers, chol, owners, branch_src):
    branched = walkers[branch_src]
    picked = chol[jnp.arange(N_VEC)[:, None], owners]
    stacked = picked.reshape(N_VEC * G_USE * NE, 2 * NORB)

    def per_walker(state):
        pbig = complex_block(state[:NORB])
        obig = complex_block(state[NORB:]).astype(jnp.float32)
        mixed = jnp.dot(stacked, pbig, preferred_element_type=jnp.float32).astype(jnp.bfloat16)
        mixed = mixed.reshape(N_VEC * G_USE, NE, 2 * NE).astype(jnp.float32)
        green = jnp.einsum('gik,kj->gij', mixed, obig, precision=lax.Precision.HIGHEST)
        real = green[:, :, :NE]
        imag = green[:, :, NE:]
        bias = jnp.stack([jnp.trace(real, axis1=1, axis2=2), jnp.trace(imag, axis1=1, axis2=2)], axis=1)
        real_t = jnp.swapaxes(real, 1, 2)
        imag_t = jnp.swapaxes(imag, 1, 2)
        ex_real = jnp.sum(real * real_t - imag * imag_t)
        ex_imag = 2.0 * jnp.sum(real * imag_t)
        return bias, -0.5 * jnp.stack([ex_real, ex_imag])

    force_bias, exchange = lax.map(per_walker, branched)
    return branched, force_bias, exchange
```

```python
import functools

import jax
import jax.numpy as jnp
from jax import lax
from jax.experimental import pallas as pl
from jax.experimental.pallas import tpu as pltpu
from jax.sharding import PartitionSpec as P

MESH = pl.DeviceIdType.MESH
CHUNKS = 24


def flip(index):
    return index + 1 - 2 * lax.rem(index, 2)


def move_kernel(
    n_walk, n_vec, flags, slots, chol, walkers, out, partner, branched,
    home, away, own, up, down, cand, sel,
    bcast_send, home_sem, away_send, away_sem, relay_send,
    up_send, up_sem, down_send, down_sem,
    x_send, x_sem, d_send, d_sem, z_send, z_sem, local_sem, g_send, g_sem, self_sem,
):
    walk, vec = lax.axis_index("walk"), lax.axis_index("vec")
    rows = n_walk // 2
    row, col = walk // 2, lax.rem(walk, 2)
    low, high = lax.rem(vec, 2), vec // 2
    highs = n_vec // 2
    hub = low == col
    chunks, depth = home.shape[0], home.shape[1]
    piece = sel.shape[1]
    per_dev = walkers.shape[0]
    flip_walk, flip_vec = flip(walk), flip(vec)
    z_next = lax.rem(row + 1 - 2 * col + rows, rows)
    z_prev = lax.rem(row - 1 + 2 * col + rows, rows)
    z_to = {"walk": z_next * 2 + col, "vec": vec}
    z_from = {"walk": z_prev * 2 + col, "vec": vec}
    across = {"walk": flip_walk, "vec": vec}
    mate = {"walk": walk, "vec": flip_vec}
    above = {"walk": walk + 2, "vec": vec}
    below = {"walk": walk - 2, "vec": vec}

    def peer(j):
        return {"walk": walk, "vec": lax.rem(vec + j, n_vec)}

    bar = pltpu.get_barrier_semaphore()

    def hello(target):
        pl.semaphore_signal(bar, inc=1, device_id=target, device_id_type=MESH)

    hello(across)
    hello(z_to)
    hello(z_from)
    for j in range(1, n_vec):
        hello(peer(j))
    pl.semaphore_wait(bar, 3 + n_vec - 1)

    def remote(src, dst, send, recv, target):
        return pltpu.make_async_remote_copy(
            src_ref=src, dst_ref=dst, send_sem=send, recv_sem=recv,
            device_id=target, device_id_type=MESH)

    def chol_rows(k):
        return chol.at[0, 0, pl.ds(pl.multiple_of(k * depth, depth), depth)]

    def own_to_home(k):
        return pltpu.make_async_copy(chol_rows(k), home.at[k], home_sem.at[k])

    def own_to_mate(k):
        return remote(chol_rows(k), home.at[k], bcast_send.at[k], home_sem.at[k], mate)

    def own_across(k):
        return remote(chol_rows(k), away.at[k], away_send.at[k], away_sem.at[k], across)

    def away_to_mate(k):
        return remote(away.at[k], away.at[k], relay_send.at[k], away_sem.at[k], mate)

    def send_up(k):
        return remote(up.at[k], up.at[k], up_send.at[k], up_sem.at[k], above)

    def send_down(k):
        return remote(down.at[k], down.at[k], down_send.at[k], down_sem.at[k], below)

    def part(half, sub):
        return pl.ds(pl.multiple_of((half * highs + sub) * piece, piece), piece)

    def sub_of(j):
        return lax.rem(high + j, highs)

    def walker_across(w, j):
        at = part(low, sub_of(j))
        return remote(walkers.at[w, at], partner.at[w, at], x_send.at[w, j], x_sem.at[w, j], across)

    def walker_mate(w, j):
        at = part(low, sub_of(j))
        return remote(partner.at[w, at], partner.at[w, at], d_send.at[w, j], d_sem.at[w, j], mate)

    far_base = col * 2 * per_dev
    near_base = (1 - col) * 2 * per_dev
    mine = part(low, high)

    def walker_z(w):
        return remote(partner.at[w, mine], cand.at[far_base + w], z_send.at[w], z_sem.at[w], z_to)

    def own_cand(w):
        return pltpu.make_async_copy(walkers.at[w, mine], cand.at[per_dev + w], local_sem.at[w])

    def near_cand(w):
        return pltpu.make_async_copy(partner.at[w, mine], cand.at[near_base + w], local_sem.at[per_dev + w])

    def gather(s, j):
        return remote(sel.at[s], branched.at[s, mine], g_send.at[s, j - 1], g_sem.at[s, j - 1], peer(j))

    def gather_self(s):
        return pltpu.make_async_copy(sel.at[s], branched.at[s, mine], self_sem.at[s])

    def each(lo, hi, f):
        def body(k, carry):
            f(k)
            return carry
        lax.fori_loop(lo, hi, body, 0)

    @pl.when(hub)
    def _():
        def start(k):
            own_to_home(k).start()
            own_to_mate(k).start()
        for w in range(per_dev):
            walker_across(w, 0).start()
        each(0, chunks, start)

    @pl.when(jnp.logical_not(hub))
    def _():
        cut = [chunks * (w + 1) // (per_dev + 1) for w in range(per_dev)]
        at = 0
        for w in range(per_dev):
            each(at, cut[w], lambda k: own_across(k).start())
            walker_across(w, 0).start()
            at = cut[w]
        each(at, chunks, lambda k: own_across(k).start())

    for j in range(1, highs):
        for w in range(per_dev):
            walker_across(w, j).start()
    for w in range(per_dev):
        own_cand(w).start()

    last = rows - 1
    here = flags[0] == 1
    below_or_here = flags[1] == 1
    from_home = flags[2] == 1

    def step(i):
        @pl.when(i < chunks)
        def _():
            @pl.when(hub)
            def _():
                own_across(i).wait_recv()
                away_to_mate(i).start()
                own_to_home(i).wait()

            @pl.when(jnp.logical_not(hub))
            def _():
                own_to_mate(i).wait_recv()
                away_to_mate(i).wait_recv()

            own[i] = jnp.where(from_home, home[i], away[i])

        ku = i - row
        kd = i - (last - row)

        @pl.when(jnp.logical_and(ku >= 0, ku < chunks))
        def _():
            @pl.when(row == 0)
            def _():
                up[ku] = own[ku]

            @pl.when(row > 0)
            def _():
                send_up(ku).wait_recv()
                up[ku] = jnp.where(here, own[ku], up[ku])

            @pl.when(row < last)
            def _():
                send_up(ku).start()

        @pl.when(jnp.logical_and(kd >= 0, kd < chunks))
        def _():
            @pl.when(row == last)
            def _():
                down[kd] = own[kd]

            @pl.when(row < last)
            def _():
                send_down(kd).wait_recv()
                down[kd] = jnp.where(here, own[kd], down[kd])

            @pl.when(row > 0)
            def _():
                send_down(kd).start()

    def arrive(w):
        walker_across(w, 0).wait_recv()
        walker_z(w).start()
        walker_mate(w, 0).start()
        near_cand(w).start()

    total = chunks + last
    at = 0
    for w in range(per_dev):
        cut = chunks * (w + 1) // (per_dev + 1) + 2
        each(at, cut, step)
        arrive(w)
        at = cut
    each(at, total, step)

    for j in range(1, highs):
        for w in range(per_dev):
            walker_across(w, j).wait_recv()
            walker_mate(w, j).start()

    def finish(k):
        out[pl.ds(pl.multiple_of(k * depth, depth), depth), :] = jnp.where(below_or_here, up[k], down[k])

    each(0, chunks, finish)

    for w in range(per_dev):
        own_cand(w).wait()
        near_cand(w).wait()
        walker_z(w).wait_recv()
    lines = 16
    for s in range(per_dev):
        index = slots[s]

        def pick(t, s=s, index=index):
            at = pl.ds(pl.multiple_of(t * lines, lines), lines)
            sel[s, at, :] = cand[index, at, :]

        each(0, piece // lines, pick)
        for j in range(1, n_vec):
            gather(s, j).start()
        gather_self(s).start()

    @pl.when(hub)
    def _():
        def ended(k):
            own_to_mate(k).wait_send()
            away_to_mate(k).wait_send()
        each(0, chunks, ended)

    @pl.when(jnp.logical_not(hub))
    def _():
        each(0, chunks, lambda k: own_across(k).wait_send())

    @pl.when(row < last)
    def _():
        each(0, chunks, lambda k: send_up(k).wait_send())

    @pl.when(row > 0)
    def _():
        each(0, chunks, lambda k: send_down(k).wait_send())

    for w in range(per_dev):
        for j in range(highs):
            walker_across(w, j).wait_send()
            walker_mate(w, j).wait()
        walker_z(w).wait_send()
    for s in range(per_dev):
        for j in range(1, n_vec):
            gather(s, j).wait()
        gather_self(s).wait()


def move(n_walk, n_vec, flags, slots, chol, walkers):
    per_dev, height, width = walkers.shape
    electrons, orbitals = chol.shape[2:]
    chunks = CHUNKS if electrons % (CHUNKS * 16) == 0 else 1
    depth = electrons // chunks
    highs = n_vec // 2
    big = pltpu.VMEM((chunks, depth, orbitals), chol.dtype)
    dma = pltpu.SemaphoreType.DMA
    any_spec = pl.BlockSpec(memory_space=pl.ANY)
    smem = pl.BlockSpec(memory_space=pltpu.SMEM)
    same = jax.ShapeDtypeStruct(walkers.shape, walkers.dtype)
    return pl.pallas_call(
        functools.partial(move_kernel, n_walk, n_vec),
        out_shape=(jax.ShapeDtypeStruct((electrons, orbitals), chol.dtype), same, same),
        in_specs=[smem, smem, any_spec, any_spec],
        out_specs=(pl.BlockSpec(memory_space=pltpu.VMEM), any_spec, any_spec),
        scratch_shapes=[
            big, big, big, big, big,
            pltpu.VMEM((3 * per_dev, height // n_vec, width), walkers.dtype),
            pltpu.VMEM((per_dev, height // n_vec, width), walkers.dtype),
        ] + [dma((chunks,))] * 9 + [
            dma((per_dev, highs)), dma((per_dev, highs)),
            dma((per_dev, highs)), dma((per_dev, highs)),
            dma((per_dev,)), dma((per_dev,)), dma((2 * per_dev,)),
            dma((per_dev, n_vec - 1)), dma((per_dev, n_vec - 1)), dma((per_dev,)),
        ],
        compiler_params=pltpu.CompilerParams(
            collective_id=0, has_side_effects=True, vmem_limit_bytes=48 * 1024 * 1024),
        name="move",
    )(flags, slots, chol, walkers)


def terms_kernel(per_dev, matrix, near, far, out):
    electrons = matrix.shape[0]
    orbitals = matrix.shape[1] // 2
    ahead = pl.program_id(0) < per_dev

    def work(state):
        a_re, a_im = matrix[:, :orbitals], matrix[:, orbitals:]
        p = state[0, :orbitals, :]
        o = state[0, orbitals:, :]
        x = jnp.dot(a_re, p, preferred_element_type=jnp.float32)
        y = jnp.dot(a_im, p, preferred_element_type=jnp.float32)
        m_re = (x[:, :electrons] - y[:, electrons:]).astype(jnp.bfloat16)
        m_im = (x[:, electrons:] + y[:, :electrons]).astype(jnp.bfloat16)
        u = jnp.dot(m_re, o, preferred_element_type=jnp.float32)
        v = jnp.dot(m_im, o, preferred_element_type=jnp.float32)
        g_re = u[:, :electrons] - v[:, electrons:]
        g_im = u[:, electrons:] + v[:, :electrons]
        t_re, t_im = g_re.T, g_im.T
        eye = (lax.broadcasted_iota(jnp.int32, g_re.shape, 0)
               == lax.broadcasted_iota(jnp.int32, g_re.shape, 1))
        values = [
            jnp.sum(jnp.where(eye, g_re, 0.0)),
            jnp.sum(jnp.where(eye, g_im, 0.0)),
            jnp.sum(g_re * t_re - g_im * t_im),
            2.0 * jnp.sum(g_re * t_im),
        ]
        lane = lax.broadcasted_iota(jnp.int32, out.shape, 2)
        row = jnp.zeros(out.shape, jnp.float32)
        for n, value in enumerate(values):
            row = jnp.where(lane == n, value, row)
        out[...] = row

    @pl.when(ahead)
    def _():
        work(near)

    @pl.when(jnp.logical_not(ahead))
    def _():
        work(far)


def terms(matrix, near, far):
    per_dev, height, width = near.shape
    return pl.pallas_call(
        functools.partial(terms_kernel, per_dev),
        grid=(2 * per_dev,),
        out_shape=jax.ShapeDtypeStruct((2 * per_dev, 8, 128), jnp.float32),
        in_specs=[
            pl.BlockSpec(matrix.shape, lambda i: (0, 0)),
            pl.BlockSpec((1, height, width), lambda i: (jnp.minimum(i, per_dev - 1), 0, 0)),
            pl.BlockSpec((1, height, width), lambda i: (jnp.maximum(i - per_dev, 0), 0, 0)),
        ],
        out_specs=pl.BlockSpec((1, 8, 128), lambda i: (i, 0, 0)),
        compiler_params=pltpu.CompilerParams(vmem_limit_bytes=56 * 1024 * 1024),
        name="terms",
    )(matrix, near, far)[:, 0, :4]


def shards(n_walk, n_vec, walkers, chol, owners, branch_src):
    per_dev = walkers.shape[0]
    walk, vec = lax.axis_index("walk"), lax.axis_index("vec")
    row, col, low = walk // 2, walk % 2, vec % 2
    swap = [(i, i + 1 - 2 * (i % 2)) for i in range(n_vec)]
    mate_roots = lax.ppermute(owners[0], "vec", swap)
    roots = jnp.where(low == col, owners[0], mate_roots)
    root = jnp.take(roots, low)
    flags = jnp.stack([root // 2 == row, root // 2 <= row, root % 2 == col]).astype(jnp.int32)
    total = per_dev * n_walk
    relative = ((branch_src - (walk - 1) * per_dev + total) % total).astype(jnp.int32)
    matrix, partner, branched = move(n_walk, n_vec, flags, relative, chol, walkers)
    values = terms(matrix, walkers, partner)
    table = lax.all_gather(values, ("walk", "vec"))
    table = table.reshape(n_walk // 2, 2, n_vec // 2, 2, 2, per_dev, 4)
    even, odd = table[:, 0], table[:, 1]
    near_first = jnp.stack([even[:, :, :, 0], odd[:, :, :, 1]], axis=2)
    far_first = jnp.stack([even[:, :, :, 1], odd[:, :, :, 0]], axis=2)
    both = jnp.stack([near_first, far_first], axis=1)
    both = jnp.transpose(both, (0, 1, 5, 2, 3, 4, 6)).reshape(total, n_vec, 2, 4)
    chosen = jnp.take(both, branch_src, axis=0)
    bias = lax.dynamic_slice_in_dim(chosen, vec, 1, axis=1)[:, 0, :, :2]
    energy = -0.5 * jnp.sum(chosen[..., 2:], axis=(1, 2))
    return (branched, bias, energy)


def solution(mesh):
    n_walk, n_vec = mesh.shape["walk"], mesh.shape["vec"]
    return jax.shard_map(
        functools.partial(shards, n_walk, n_vec),
        mesh=mesh,
        in_specs=(P("walk", None, None), P("vec", "walk", None, None), P("vec", None), P("walk")),
        out_specs=(P("walk", None, None), P("walk", "vec", None), P("walk", None)),
        check_vma=False,
    )
```

```python
import functools

import jax
import jax.numpy as jnp
from jax import lax
from jax.experimental import pallas as pl
from jax.experimental.pallas import tpu as pltpu
from jax.sharding import PartitionSpec as P

MESH = pl.DeviceIdType.MESH
CHUNKS = 24
PARTS = 2
EARLY = (5, 9, 12, 15)


def flip(index):
    return index + 1 - 2 * lax.rem(index, 2)


def walker_values(matrix, state):
    electrons = matrix.shape[0]
    orbitals = matrix.shape[1] // 2
    p = state[:orbitals, :]
    o = state[orbitals:, :]
    x = jnp.dot(matrix[:, :orbitals], p, preferred_element_type=jnp.float32)
    y = jnp.dot(matrix[:, orbitals:], p, preferred_element_type=jnp.float32)
    m_re = (x[:, :electrons] - y[:, electrons:]).astype(jnp.bfloat16)
    m_im = (x[:, electrons:] + y[:, :electrons]).astype(jnp.bfloat16)
    u = jnp.dot(m_re, o, preferred_element_type=jnp.float32)
    v = jnp.dot(m_im, o, preferred_element_type=jnp.float32)
    g_re = u[:, :electrons] - v[:, electrons:]
    g_im = u[:, electrons:] + v[:, :electrons]
    t_re, t_im = g_re.T, g_im.T
    eye = (lax.broadcasted_iota(jnp.int32, g_re.shape, 0)
           == lax.broadcasted_iota(jnp.int32, g_re.shape, 1))
    return [
        jnp.sum(jnp.where(eye, g_re, 0.0)),
        jnp.sum(jnp.where(eye, g_im, 0.0)),
        jnp.sum(g_re * t_re - g_im * t_im),
        2.0 * jnp.sum(g_re * t_im),
    ]


def step_kernel(
    n_walk, n_vec, flags, slots, chol, walkers, table, partner, branched,
    home, away, own, up, down, cand_0, cand_1, sel, matrix, state, result,
    bcast_send, home_sem, away_send, away_sem, relay_send,
    up_send, up_sem, down_send, down_sem,
    x_send, x_sem, z_send, z_sem, local_sem,
    y_send, y_sem, d_send, d_sem, r_send, r_sem,
    by_send, by_sem, bd_send, bd_sem, br_send, br_sem, self_sem,
    load_sem, t_send, t_sem,
):
    walk, vec = lax.axis_index("walk"), lax.axis_index("vec")
    rows = n_walk // 2
    row, col = walk // 2, lax.rem(walk, 2)
    low = lax.rem(vec, 2)
    hub = low == col
    cand = (cand_0, cand_1)
    chunks, depth = home.shape[0], home.shape[1]
    per_dev = walkers.shape[0]
    quarter = sel.shape[1]
    piece = quarter // PARTS
    pieces = [(w, t) for t in range(PARTS) for w in range(per_dev)]
    flip_walk, flip_vec = flip(walk), flip(vec)
    far_vec = lax.rem(vec + 2, n_vec)
    z_next = lax.rem(row + 1 - 2 * col + rows, rows)
    z_to = {"walk": z_next * 2 + col, "vec": vec}
    across = {"walk": flip_walk, "vec": vec}
    mate = {"walk": walk, "vec": flip_vec}
    over = {"walk": walk, "vec": far_vec}
    above = {"walk": walk + 2, "vec": vec}
    below = {"walk": walk - 2, "vec": vec}
    row_up, row_down = lax.rem(row + 1, rows), lax.rem(row + rows - 1, rows)

    place = col * n_vec + vec
    readers = [({"walk": walk, "vec": lax.rem(vec + j, n_vec)}, place) for j in range(1, n_vec)]
    readers += [({"walk": flip_walk, "vec": lax.rem(vec + j, n_vec)}, place) for j in range(n_vec)]
    readers += [({"walk": row_up * 2, "vec": lax.rem(vec + j, n_vec)}, place + 2 * n_vec) for j in range(n_vec)]
    readers += [({"walk": row_down * 2 + 1, "vec": lax.rem(vec + j, n_vec)}, place + 2 * n_vec) for j in range(n_vec)]

    bar = pltpu.get_barrier_semaphore()
    for target in (
        [t for t, _ in readers[:2 * n_vec - 1]]
        + [{"walk": r * 2 + c, "vec": lax.rem(vec + j, n_vec)}
           for r in (row_up, row_down) for c in range(2) for j in range(n_vec)]
    ):
        pl.semaphore_signal(bar, inc=1, device_id=target, device_id_type=MESH)
    pl.semaphore_wait(bar, 6 * n_vec - 1)

    def remote(src, dst, send, recv, target):
        return pltpu.make_async_remote_copy(
            src_ref=src, dst_ref=dst, send_sem=send, recv_sem=recv,
            device_id=target, device_id_type=MESH)

    def chol_rows(k):
        return chol.at[0, 0, pl.ds(pl.multiple_of(k * depth, depth), depth)]

    def own_to_home(k):
        return pltpu.make_async_copy(chol_rows(k), home.at[k], home_sem.at[k])

    def own_to_mate(k):
        return remote(chol_rows(k), home.at[k], bcast_send.at[k], home_sem.at[k], mate)

    def own_across(k):
        return remote(chol_rows(k), away.at[k], away_send.at[k], away_sem.at[k], across)

    def away_to_mate(k):
        return remote(away.at[k], away.at[k], relay_send.at[k], away_sem.at[k], mate)

    def send_up(k):
        return remote(up.at[k], up.at[k], up_send.at[k], up_sem.at[k], above)

    def send_down(k):
        return remote(down.at[k], down.at[k], down_send.at[k], down_sem.at[k], below)

    def part(index, t):
        return pl.ds(pl.multiple_of(index * quarter + t * piece, piece), piece)

    def inner(t):
        return pl.ds(t * piece, piece)

    far_base = col * 2 * per_dev
    near_base = (1 - col) * 2 * per_dev

    def walker_across(w, t):
        at = part(vec, t)
        return remote(walkers.at[w, at], partner.at[w, at], x_send.at[w, t], x_sem.at[w, t], across)

    def walker_z(w, t):
        return remote(partner.at[w, part(vec, t)], cand[t].at[far_base + w],
                      z_send.at[w, t], z_sem.at[w, t], z_to)

    def own_cand(w, t):
        return pltpu.make_async_copy(
            walkers.at[w, part(vec, t)], cand[t].at[per_dev + w], local_sem.at[w, t])

    def near_cand(w, t):
        return pltpu.make_async_copy(
            partner.at[w, part(vec, t)], cand[t].at[near_base + w], local_sem.at[w, PARTS + t])

    def walker_y(w, t):
        at = part(vec, t)
        return remote(partner.at[w, at], partner.at[w, at], y_send.at[w, t], y_sem.at[w, t], over)

    def walker_mate(w, t):
        at = part(vec, t)
        return remote(partner.at[w, at], partner.at[w, at], d_send.at[w, t], d_sem.at[w, t], mate)

    def walker_relay(w, t):
        at = part(far_vec, t)
        return remote(partner.at[w, at], partner.at[w, at], r_send.at[w, t], r_sem.at[w, t], mate)

    def slot_y(s, t):
        return remote(sel.at[s, inner(t)], branched.at[s, part(vec, t)], by_send.at[s, t], by_sem.at[s, t], over)

    def slot_mate(s, t):
        return remote(sel.at[s, inner(t)], branched.at[s, part(vec, t)], bd_send.at[s, t], bd_sem.at[s, t], mate)

    def slot_relay(s, t):
        at = part(far_vec, t)
        return remote(branched.at[s, at], branched.at[s, at], br_send.at[s, t], br_sem.at[s, t], mate)

    def slot_self(s, t):
        return pltpu.make_async_copy(sel.at[s, inner(t)], branched.at[s, part(vec, t)], self_sem.at[s, t])

    def each(lo, hi, f):
        def body(k, carry):
            f(k)
            return carry
        lax.fori_loop(lo, hi, body, 0)

    for w, t in pieces:
        own_cand(w, t).start()

    @pl.when(hub)
    def _():
        def start(k):
            own_to_home(k).start()
            own_to_mate(k).start()
        for w, t in pieces:
            walker_across(w, t).start()
        each(0, chunks, start)

    @pl.when(jnp.logical_not(hub))
    def _():
        each(0, chunks, lambda k: own_across(k).start())
        for w, t in pieces:
            walker_across(w, t).start()

    for w in range(per_dev):
        pltpu.make_async_copy(walkers.at[w], state.at[w], load_sem.at[w]).start()

    last = rows - 1
    here = flags[0] == 1
    below_or_here = flags[1] == 1
    from_home = flags[2] == 1

    def step(i):
        @pl.when(i < chunks)
        def _():
            @pl.when(hub)
            def _():
                own_across(i).wait_recv()
                away_to_mate(i).start()
                own_to_home(i).wait()

            @pl.when(jnp.logical_not(hub))
            def _():
                own_to_mate(i).wait_recv()
                away_to_mate(i).wait_recv()

            own[i] = jnp.where(from_home, home[i], away[i])

        ku = i - row
        kd = i - (last - row)

        @pl.when(jnp.logical_and(ku >= 0, ku < chunks))
        def _():
            @pl.when(row == 0)
            def _():
                up[ku] = own[ku]

            @pl.when(row > 0)
            def _():
                send_up(ku).wait_recv()
                up[ku] = jnp.where(here, own[ku], up[ku])

            @pl.when(row < last)
            def _():
                send_up(ku).start()

        @pl.when(jnp.logical_and(kd >= 0, kd < chunks))
        def _():
            @pl.when(row == last)
            def _():
                down[kd] = own[kd]

            @pl.when(row < last)
            def _():
                send_down(kd).wait_recv()
                down[kd] = jnp.where(here, own[kd], down[kd])

            @pl.when(row > 0)
            def _():
                send_down(kd).start()

    def arrive(w, t):
        walker_across(w, t).wait_recv()
        walker_z(w, t).start()
        walker_y(w, t).start()
        walker_mate(w, t).start()
        near_cand(w, t).start()

    total = chunks + last
    at = 0
    for n, (w, t) in enumerate(pieces):
        cut = min(EARLY[min(n, len(EARLY) - 1)], total)
        each(at, cut, step)
        at = cut

        @pl.when(jnp.logical_not(hub))
        def _():
            arrive(w, t)
    each(at, total, step)

    @pl.when(hub)
    def _():
        for w, t in pieces:
            arrive(w, t)

    def finish(k):
        matrix[pl.ds(pl.multiple_of(k * depth, depth), depth), :] = jnp.where(below_or_here, up[k], down[k])

    each(0, chunks, finish)

    lines = 16

    def select(t):
        for w in range(per_dev):
            near_cand(w, t).wait()
            walker_z(w, t).wait_recv()
        for s in range(per_dev):
            index = slots[s]

            def pick(n, s=s, index=index):
                at = pl.ds(pl.multiple_of(t * piece + n * lines, lines), lines)
                sel[s, at, :] = cand[t][index, pl.ds(pl.multiple_of(n * lines, lines), lines), :]

            each(0, piece // lines, pick)
            slot_y(s, t).start()
            slot_mate(s, t).start()
            slot_self(s, t).start()

    for w, t in pieces:
        own_cand(w, t).wait()

    @pl.when(jnp.logical_not(hub))
    def _():
        for t in range(PARTS):
            select(t)

    for w, t in pieces:
        walker_y(w, t).wait_recv()
        walker_relay(w, t).start()
    for w, t in pieces:
        walker_mate(w, t).wait_recv()
        walker_relay(w, t).wait_recv()

    def load(i):
        return pltpu.make_async_copy(partner.at[i], state.at[i], load_sem.at[i])

    sub = lax.broadcasted_iota(jnp.int32, result.shape, 0)
    lane = lax.broadcasted_iota(jnp.int32, result.shape, 1)
    result[...] = jnp.zeros_like(result)

    def compute(i):
        slot = lax.rem(i, per_dev)
        load(slot).wait()
        for n, value in enumerate(walker_values(matrix, state.at[slot])):
            result[...] = jnp.where(jnp.logical_and(sub == i, lane == n), value, result[...])

        @pl.when(i < per_dev)
        def _():
            load(slot).start()

    each(0, 2 * per_dev, compute)

    def tell(n):
        target, where = readers[n]
        return remote(result, table.at[where], t_send.at[n], t_sem.at[where], target)

    for n in range(len(readers)):
        tell(n).start()

    @pl.when(hub)
    def _():
        for t in range(PARTS):
            select(t)

    table[place] = result[...]

    for t in range(PARTS):
        for s in range(per_dev):
            slot_y(s, t).wait_recv()
            slot_relay(s, t).start()

    @pl.when(hub)
    def _():
        def ended(k):
            own_to_mate(k).wait_send()
            away_to_mate(k).wait_send()
        each(0, chunks, ended)

    @pl.when(jnp.logical_not(hub))
    def _():
        each(0, chunks, lambda k: own_across(k).wait_send())

    @pl.when(row < last)
    def _():
        each(0, chunks, lambda k: send_up(k).wait_send())

    @pl.when(row > 0)
    def _():
        each(0, chunks, lambda k: send_down(k).wait_send())

    for w, t in pieces:
        walker_across(w, t).wait_send()
        walker_z(w, t).wait_send()
        walker_y(w, t).wait_send()
        walker_mate(w, t).wait_send()
        walker_relay(w, t).wait_send()
    for n in range(len(readers)):
        tell(n).wait_send()

    for j in range(1, n_vec):
        v = lax.rem(vec + j, n_vec)
        remote(result, table.at[0], t_send.at[0], t_sem.at[col * n_vec + v], mate).wait_recv()
    for j in range(n_vec):
        remote(result, table.at[0], t_send.at[0], t_sem.at[(1 - col) * n_vec + j], mate).wait_recv()
    for j in range(2 * n_vec):
        remote(result, table.at[0], t_send.at[0], t_sem.at[2 * n_vec + j], mate).wait_recv()

    for t in range(PARTS):
        for s in range(per_dev):
            slot_y(s, t).wait_send()
            slot_mate(s, t).wait()
            slot_relay(s, t).wait()
            slot_self(s, t).wait()


def step_all(n_walk, n_vec, flags, slots, chol, walkers):
    per_dev, height, width = walkers.shape
    electrons, orbitals = chol.shape[2:]
    chunks = CHUNKS if electrons % (CHUNKS * 16) == 0 else 1
    depth = electrons // chunks
    big = pltpu.VMEM((chunks, depth, orbitals), chol.dtype)
    dma = pltpu.SemaphoreType.DMA
    any_spec = pl.BlockSpec(memory_space=pl.ANY)
    smem = pl.BlockSpec(memory_space=pltpu.SMEM)
    same = jax.ShapeDtypeStruct(walkers.shape, walkers.dtype)
    piece_sem = dma((per_dev, PARTS))
    return pl.pallas_call(
        functools.partial(step_kernel, n_walk, n_vec),
        out_shape=(jax.ShapeDtypeStruct((4 * n_vec, 8, 128), jnp.float32), same, same),
        in_specs=[smem, smem, any_spec, any_spec],
        out_specs=(pl.BlockSpec(memory_space=pltpu.VMEM), any_spec, any_spec),
        scratch_shapes=[
            big, big, big, big, big,
            pltpu.VMEM((3 * per_dev, height // n_vec // PARTS, width), walkers.dtype),
            pltpu.VMEM((3 * per_dev, height // n_vec // PARTS, width), walkers.dtype),
            pltpu.VMEM((per_dev, height // n_vec, width), walkers.dtype),
            pltpu.VMEM((electrons, orbitals), chol.dtype),
            pltpu.VMEM((per_dev, height, width), walkers.dtype),
            pltpu.VMEM((8, 128), jnp.float32),
        ] + [dma((chunks,))] * 9 + [piece_sem] * 4 + [dma((per_dev, 2 * PARTS))]
        + [piece_sem] * 13 + [dma((per_dev,)), dma((4 * n_vec - 1,)), dma((4 * n_vec,))],
        compiler_params=pltpu.CompilerParams(
            collective_id=0, has_side_effects=True, vmem_limit_bytes=60 * 1024 * 1024),
        name="step_all",
    )(flags, slots, chol, walkers)


def shards(n_walk, n_vec, walkers, chol, owners, branch_src):
    per_dev = walkers.shape[0]
    walk, vec = lax.axis_index("walk"), lax.axis_index("vec")
    row, col, low = walk // 2, walk % 2, vec % 2
    swap = [(i, i + 1 - 2 * (i % 2)) for i in range(n_vec)]
    mate_roots = lax.ppermute(owners[0], "vec", swap)
    roots = jnp.where(low == col, owners[0], mate_roots)
    root = jnp.take(roots, low)
    flags = jnp.stack([root // 2 == row, root // 2 <= row, root % 2 == col]).astype(jnp.int32)
    total = per_dev * n_walk
    relative = ((branch_src - (walk - 1) * per_dev + total) % total).astype(jnp.int32)
    table, _, branched = step_all(n_walk, n_vec, flags, relative, chol, walkers)
    table = table[:, :2 * per_dev, :4].reshape(2, 2, n_vec // 2, 2, 2, per_dev, 4)
    even, odd = table[:, 0], table[:, 1]
    first = jnp.stack([even[:, :, :, 0], odd[:, :, :, 1]], axis=2)
    second = jnp.stack([even[:, :, :, 1], odd[:, :, :, 0]], axis=2)
    both = jnp.stack([first, second], axis=1)
    both = jnp.transpose(both, (0, 1, 5, 2, 3, 4, 6)).reshape(4 * per_dev, n_vec, 2, 4)
    side = relative // per_dev
    block = jnp.where(side == 1, col, jnp.where(side == 2 * (1 - col), 1 - col, 3 - col))
    chosen = jnp.take(both, block * per_dev + relative % per_dev, axis=0)
    bias = lax.dynamic_slice_in_dim(chosen, vec, 1, axis=1)[:, 0, :, :2]
    energy = -0.5 * jnp.sum(chosen[..., 2:], axis=(1, 2))
    return (branched, bias, energy)


def solution(mesh):
    n_walk, n_vec = mesh.shape["walk"], mesh.shape["vec"]
    return jax.shard_map(
        functools.partial(shards, n_walk, n_vec),
        mesh=mesh,
        in_specs=(P("walk", None, None), P("vec", "walk", None, None), P("vec", None), P("walk")),
        out_specs=(P("walk", None, None), P("walk", "vec", None), P("walk", None)),
        check_vma=False,
    )
```

```python
import functools

import jax
import jax.numpy as jnp
from jax import lax
from jax.experimental import pallas as pl
from jax.experimental.pallas import tpu as pltpu
from jax.sharding import PartitionSpec as P

MESH = pl.DeviceIdType.MESH
CHUNKS = 24
PARTS = 2
SKEW = 3
AHEAD = 3
QUEUE = (12, 15, 18, 21)
LEAF = ((5, 9, 12, 15), (9, 13, 16, 19), (17, 24), (24, 100))
HUB = ((18, 22, 26, 30), (22, 26, 30, 100), (100, 200), (200, 200))


def flip(index):
    return index + 1 - 2 * lax.rem(index, 2)


def walker_values(matrix, state):
    electrons = matrix.shape[0]
    orbitals = matrix.shape[1] // 2
    p = state[:orbitals, :]
    o = state[orbitals:, :]
    x = jnp.dot(matrix[:, :orbitals], p, preferred_element_type=jnp.float32)
    y = jnp.dot(matrix[:, orbitals:], p, preferred_element_type=jnp.float32)
    m_re = (x[:, :electrons] - y[:, electrons:]).astype(jnp.bfloat16)
    m_im = (x[:, electrons:] + y[:, :electrons]).astype(jnp.bfloat16)
    u = jnp.dot(m_re, o, preferred_element_type=jnp.float32)
    v = jnp.dot(m_im, o, preferred_element_type=jnp.float32)
    g_re = u[:, :electrons] - v[:, electrons:]
    g_im = u[:, electrons:] + v[:, :electrons]
    t_re, t_im = g_re.T, g_im.T
    eye = (lax.broadcasted_iota(jnp.int32, g_re.shape, 0)
           == lax.broadcasted_iota(jnp.int32, g_re.shape, 1))
    return [
        jnp.sum(jnp.where(eye, g_re, 0.0)),
        jnp.sum(jnp.where(eye, g_im, 0.0)),
        jnp.sum(g_re * t_re - g_im * t_im),
        2.0 * jnp.sum(g_re * t_im),
    ]


def step_kernel(
    n_walk, n_vec, flags, slots, chol, walkers, table, partner, branched,
    home, away, own, up, down, cand_0, cand_1, sel, matrix, state, result,
    bcast_send, home_sem, away_send, away_sem, relay_send,
    up_send, up_sem, down_send, down_sem,
    x_send, x_sem, z_send, z_sem, local_sem,
    y_send, y_sem, d_send, d_sem, r_send, r_sem,
    by_send, by_sem, bd_send, bd_sem, br_send, br_sem, self_sem,
    load_sem, t_send, t_sem,
):
    walk, vec = lax.axis_index("walk"), lax.axis_index("vec")
    rows = n_walk // 2
    row, col = walk // 2, lax.rem(walk, 2)
    low = lax.rem(vec, 2)
    hub = low == col
    cand = (cand_0, cand_1)
    chunks, depth = home.shape[0], home.shape[1]
    per_dev = walkers.shape[0]
    quarter = sel.shape[1]
    piece = quarter // PARTS
    pieces = [(w, t) for t in range(PARTS) for w in range(per_dev)]
    flip_walk, flip_vec = flip(walk), flip(vec)
    far_vec = lax.rem(vec + 2, n_vec)
    z_next = lax.rem(row + 1 - 2 * col + rows, rows)
    z_to = {"walk": z_next * 2 + col, "vec": vec}
    across = {"walk": flip_walk, "vec": vec}
    mate = {"walk": walk, "vec": flip_vec}
    over = {"walk": walk, "vec": far_vec}
    above = {"walk": walk + 2, "vec": vec}
    below = {"walk": walk - 2, "vec": vec}
    row_up, row_down = lax.rem(row + 1, rows), lax.rem(row + rows - 1, rows)

    place = col * n_vec + vec
    readers = [({"walk": walk, "vec": lax.rem(vec + j, n_vec)}, place) for j in range(1, n_vec)]
    readers += [({"walk": flip_walk, "vec": lax.rem(vec + j, n_vec)}, place) for j in range(n_vec)]
    readers += [({"walk": row_up * 2, "vec": lax.rem(vec + j, n_vec)}, place + 2 * n_vec) for j in range(n_vec)]
    readers += [({"walk": row_down * 2 + 1, "vec": lax.rem(vec + j, n_vec)}, place + 2 * n_vec) for j in range(n_vec)]

    bar = pltpu.get_barrier_semaphore()
    for target in (
        [t for t, _ in readers[:2 * n_vec - 1]]
        + [{"walk": r * 2 + c, "vec": lax.rem(vec + j, n_vec)}
           for r in (row_up, row_down) for c in range(2) for j in range(n_vec)]
    ):
        pl.semaphore_signal(bar, inc=1, device_id=target, device_id_type=MESH)
    pl.semaphore_wait(bar, 6 * n_vec - 1)

    def remote(src, dst, send, recv, target):
        return pltpu.make_async_remote_copy(
            src_ref=src, dst_ref=dst, send_sem=send, recv_sem=recv,
            device_id=target, device_id_type=MESH)

    def chol_rows(k):
        return chol.at[0, 0, pl.ds(pl.multiple_of(k * depth, depth), depth)]

    def own_to_home(k):
        return pltpu.make_async_copy(chol_rows(k), home.at[k], home_sem.at[k])

    def own_to_mate(k):
        return remote(chol_rows(k), home.at[k], bcast_send.at[k], home_sem.at[k], mate)

    def own_across(k):
        return remote(chol_rows(k), away.at[k], away_send.at[k], away_sem.at[k], across)

    def away_to_mate(k):
        return remote(away.at[k], away.at[k], relay_send.at[k], away_sem.at[k], mate)

    def send_up(k):
        return remote(up.at[k], up.at[k], up_send.at[k], up_sem.at[k], above)

    def send_down(k):
        return remote(down.at[k], down.at[k], down_send.at[k], down_sem.at[k], below)

    def part(index, t):
        return pl.ds(pl.multiple_of(index * quarter + t * piece, piece), piece)

    def inner(t):
        return pl.ds(t * piece, piece)

    far_base = col * 2 * per_dev
    near_base = (1 - col) * 2 * per_dev

    def walker_across(w, t):
        at = part(vec, t)
        return remote(walkers.at[w, at], partner.at[w, at], x_send.at[w, t], x_sem.at[w, t], across)

    def walker_z(w, t):
        return remote(partner.at[w, part(vec, t)], cand[t].at[far_base + w],
                      z_send.at[w, t], z_sem.at[w, t], z_to)

    def own_cand(w, t):
        return pltpu.make_async_copy(
            walkers.at[w, part(vec, t)], cand[t].at[per_dev + w], local_sem.at[w, t])

    def near_cand(w, t):
        return pltpu.make_async_copy(
            partner.at[w, part(vec, t)], cand[t].at[near_base + w], local_sem.at[w, PARTS + t])

    def walker_y(w, t):
        at = part(vec, t)
        return remote(partner.at[w, at], partner.at[w, at], y_send.at[w, t], y_sem.at[w, t], over)

    def walker_mate(w, t):
        at = part(vec, t)
        return remote(partner.at[w, at], partner.at[w, at], d_send.at[w, t], d_sem.at[w, t], mate)

    def walker_relay(w, t):
        at = part(far_vec, t)
        return remote(partner.at[w, at], partner.at[w, at], r_send.at[w, t], r_sem.at[w, t], mate)

    def slot_y(s, t):
        return remote(sel.at[s, inner(t)], branched.at[s, part(vec, t)], by_send.at[s, t], by_sem.at[s, t], over)

    def slot_mate(s, t):
        return remote(sel.at[s, inner(t)], branched.at[s, part(vec, t)], bd_send.at[s, t], bd_sem.at[s, t], mate)

    def slot_relay(s, t):
        at = part(far_vec, t)
        return remote(branched.at[s, at], branched.at[s, at], br_send.at[s, t], br_sem.at[s, t], mate)

    def slot_self(s, t):
        return pltpu.make_async_copy(sel.at[s, inner(t)], branched.at[s, part(vec, t)], self_sem.at[s, t])

    def each(lo, hi, f):
        def body(k, carry):
            f(k)
            return carry
        lax.fori_loop(lo, hi, body, 0)

    for w, t in pieces:
        own_cand(w, t).start()

    @pl.when(hub)
    def _():
        def start(k):
            own_to_home(k).start()

            @pl.when(k < AHEAD)
            def _():
                own_to_mate(k).start()

        for w, t in pieces:
            walker_across(w, t).start()
        each(0, chunks, start)

    @pl.when(jnp.logical_not(hub))
    def _():
        at = 0
        for n, (w, t) in enumerate(pieces):
            cut = min(QUEUE[min(n, len(QUEUE) - 1)], chunks)
            each(at, cut, lambda k: own_across(k).start())
            walker_across(w, t).start()
            at = cut
        each(at, chunks, lambda k: own_across(k).start())

    for w in range(per_dev):
        pltpu.make_async_copy(walkers.at[w], state.at[w], load_sem.at[w]).start()

    last = rows - 1
    here = flags[0] == 1
    below_or_here = flags[1] == 1
    from_home = flags[2] == 1

    def step(i):
        @pl.when(i < chunks)
        def _():
            @pl.when(hub)
            def _():
                own_across(i).wait_recv()
                away_to_mate(i).start()

                @pl.when(i + AHEAD < chunks)
                def _():
                    own_to_mate(i + AHEAD).start()

                own_to_home(i).wait()

            @pl.when(jnp.logical_not(hub))
            def _():
                own_to_mate(i).wait_recv()
                away_to_mate(i).wait_recv()

            own[i] = jnp.where(from_home, home[i], away[i])

        ku = i - SKEW * row
        kd = i - SKEW * (last - row)

        @pl.when(jnp.logical_and(ku >= 0, ku < chunks))
        def _():
            @pl.when(row == 0)
            def _():
                up[ku] = own[ku]

            @pl.when(row > 0)
            def _():
                send_up(ku).wait_recv()
                up[ku] = jnp.where(here, own[ku], up[ku])

            @pl.when(row < last)
            def _():
                send_up(ku).start()

        @pl.when(jnp.logical_and(kd >= 0, kd < chunks))
        def _():
            @pl.when(row == last)
            def _():
                down[kd] = own[kd]

            @pl.when(row < last)
            def _():
                send_down(kd).wait_recv()
                down[kd] = jnp.where(here, own[kd], down[kd])

            @pl.when(row > 0)
            def _():
                send_down(kd).start()

    def arrive(w, t):
        walker_across(w, t).wait_recv()
        walker_z(w, t).start()
        walker_y(w, t).start()
        walker_mate(w, t).start()
        near_cand(w, t).start()

    lines = 16

    def select(t):
        for w in range(per_dev):
            own_cand(w, t).wait()
            near_cand(w, t).wait()
            walker_z(w, t).wait_recv()
        for s in range(per_dev):
            index = slots[s]

            def pick(n, s=s, index=index):
                at = pl.ds(pl.multiple_of(t * piece + n * lines, lines), lines)
                sel[s, at, :] = cand[t][index, pl.ds(pl.multiple_of(n * lines, lines), lines), :]

            each(0, piece // lines, pick)
            slot_y(s, t).start()
            slot_mate(s, t).start()
            slot_self(s, t).start()

    def pass_on(w, t):
        walker_y(w, t).wait_recv()
        walker_relay(w, t).start()

    def pass_slots(t):
        for s in range(per_dev):
            slot_y(s, t).wait_recv()
            slot_relay(s, t).start()

    events = []
    for times, role in ((LEAF, jnp.logical_not(hub)), (HUB, hub)):
        for n, (w, t) in enumerate(pieces):
            n = min(n, len(times[0]) - 1)
            events.append((times[0][n], role, functools.partial(arrive, w, t)))
            events.append((times[1][n], role, functools.partial(pass_on, w, t)))
        for t in range(PARTS):
            events.append((times[2][t], role, functools.partial(select, t)))
            events.append((times[3][t], role, functools.partial(pass_slots, t)))
    events.sort(key=lambda event: event[0])

    def run(event):
        @pl.when(event[1])
        def _():
            event[2]()

    total = chunks + SKEW * last
    at = 0
    for event in events:
        if event[0] < 200:
            cut = min(event[0], total)
            if cut > at:
                each(at, cut, step)
                at = cut
            run(event)
    each(at, total, step)

    def finish(k):
        matrix[pl.ds(pl.multiple_of(k * depth, depth), depth), :] = jnp.where(below_or_here, up[k], down[k])

    each(0, chunks, finish)

    for w, t in pieces:
        walker_mate(w, t).wait_recv()
        walker_relay(w, t).wait_recv()

    def load(i):
        return pltpu.make_async_copy(partner.at[i], state.at[i], load_sem.at[i])

    sub = lax.broadcasted_iota(jnp.int32, result.shape, 0)
    lane = lax.broadcasted_iota(jnp.int32, result.shape, 1)
    result[...] = jnp.zeros_like(result)

    def compute(i):
        slot = lax.rem(i, per_dev)
        load(slot).wait()
        for n, value in enumerate(walker_values(matrix, state.at[slot])):
            result[...] = jnp.where(jnp.logical_and(sub == i, lane == n), value, result[...])

        @pl.when(i < per_dev)
        def _():
            load(slot).start()

    each(0, 2 * per_dev, compute)

    def tell(n):
        target, where = readers[n]
        return remote(result, table.at[where], t_send.at[n], t_sem.at[where], target)

    for n in range(len(readers)):
        tell(n).start()

    for event in events:
        if event[0] >= 200:
            run(event)

    table[place] = result[...]

    @pl.when(hub)
    def _():
        def ended(k):
            own_to_mate(k).wait_send()
            away_to_mate(k).wait_send()
        each(0, chunks, ended)

    @pl.when(jnp.logical_not(hub))
    def _():
        each(0, chunks, lambda k: own_across(k).wait_send())

    @pl.when(row < last)
    def _():
        each(0, chunks, lambda k: send_up(k).wait_send())

    @pl.when(row > 0)
    def _():
        each(0, chunks, lambda k: send_down(k).wait_send())

    for w, t in pieces:
        walker_across(w, t).wait_send()
        walker_z(w, t).wait_send()
        walker_y(w, t).wait_send()
        walker_mate(w, t).wait_send()
        walker_relay(w, t).wait_send()
    for n in range(len(readers)):
        tell(n).wait_send()

    for j in range(1, n_vec):
        v = lax.rem(vec + j, n_vec)
        remote(result, table.at[0], t_send.at[0], t_sem.at[col * n_vec + v], mate).wait_recv()
    for j in range(n_vec):
        remote(result, table.at[0], t_send.at[0], t_sem.at[(1 - col) * n_vec + j], mate).wait_recv()
    for j in range(2 * n_vec):
        remote(result, table.at[0], t_send.at[0], t_sem.at[2 * n_vec + j], mate).wait_recv()

    for t in range(PARTS):
        for s in range(per_dev):
            slot_y(s, t).wait_send()
            slot_mate(s, t).wait()
            slot_relay(s, t).wait()
            slot_self(s, t).wait()


def step_all(n_walk, n_vec, flags, slots, chol, walkers):
    per_dev, height, width = walkers.shape
    electrons, orbitals = chol.shape[2:]
    chunks = CHUNKS if electrons % (CHUNKS * 16) == 0 else 1
    depth = electrons // chunks
    big = pltpu.VMEM((chunks, depth, orbitals), chol.dtype)
    dma = pltpu.SemaphoreType.DMA
    any_spec = pl.BlockSpec(memory_space=pl.ANY)
    smem = pl.BlockSpec(memory_space=pltpu.SMEM)
    same = jax.ShapeDtypeStruct(walkers.shape, walkers.dtype)
    piece_sem = dma((per_dev, PARTS))
    return pl.pallas_call(
        functools.partial(step_kernel, n_walk, n_vec),
        out_shape=(jax.ShapeDtypeStruct((4 * n_vec, 8, 128), jnp.float32), same, same),
        in_specs=[smem, smem, any_spec, any_spec],
        out_specs=(pl.BlockSpec(memory_space=pltpu.VMEM), any_spec, any_spec),
        scratch_shapes=[
            big, big, big, big, big,
            pltpu.VMEM((3 * per_dev, height // n_vec // PARTS, width), walkers.dtype),
            pltpu.VMEM((3 * per_dev, height // n_vec // PARTS, width), walkers.dtype),
            pltpu.VMEM((per_dev, height // n_vec, width), walkers.dtype),
            pltpu.VMEM((electrons, orbitals), chol.dtype),
            pltpu.VMEM((per_dev, height, width), walkers.dtype),
            pltpu.VMEM((8, 128), jnp.float32),
        ] + [dma((chunks,))] * 9 + [piece_sem] * 4 + [dma((per_dev, 2 * PARTS))]
        + [piece_sem] * 13 + [dma((per_dev,)), dma((4 * n_vec - 1,)), dma((4 * n_vec,))],
        compiler_params=pltpu.CompilerParams(
            collective_id=0, has_side_effects=True, vmem_limit_bytes=60 * 1024 * 1024),
        name="step_all",
    )(flags, slots, chol, walkers)


def shards(n_walk, n_vec, walkers, chol, owners, branch_src):
    per_dev = walkers.shape[0]
    walk, vec = lax.axis_index("walk"), lax.axis_index("vec")
    row, col, low = walk // 2, walk % 2, vec % 2
    swap = [(i, i + 1 - 2 * (i % 2)) for i in range(n_vec)]
    mate_roots = lax.ppermute(owners[0], "vec", swap)
    roots = jnp.where(low == col, owners[0], mate_roots)
    root = jnp.take(roots, low)
    flags = jnp.stack([root // 2 == row, root // 2 <= row, root % 2 == col]).astype(jnp.int32)
    total = per_dev * n_walk
    relative = ((branch_src - (walk - 1) * per_dev + total) % total).astype(jnp.int32)
    table, _, branched = step_all(n_walk, n_vec, flags, relative, chol, walkers)
    table = table[:, :2 * per_dev, :4].reshape(2, 2, n_vec // 2, 2, 2, per_dev, 4)
    even, odd = table[:, 0], table[:, 1]
    first = jnp.stack([even[:, :, :, 0], odd[:, :, :, 1]], axis=2)
    second = jnp.stack([even[:, :, :, 1], odd[:, :, :, 0]], axis=2)
    both = jnp.stack([first, second], axis=1)
    both = jnp.transpose(both, (0, 1, 5, 2, 3, 4, 6)).reshape(4 * per_dev, n_vec, 2, 4)
    side = relative // per_dev
    block = jnp.where(side == 1, col, jnp.where(side == 2 * (1 - col), 1 - col, 3 - col))
    chosen = jnp.take(both, block * per_dev + relative % per_dev, axis=0)
    bias = lax.dynamic_slice_in_dim(chosen, vec, 1, axis=1)[:, 0, :, :2]
    energy = -0.5 * jnp.sum(chosen[..., 2:], axis=(1, 2))
    return (branched, bias, energy)


def solution(mesh):
    n_walk, n_vec = mesh.shape["walk"], mesh.shape["vec"]
    return jax.shard_map(
        functools.partial(shards, n_walk, n_vec),
        mesh=mesh,
        in_specs=(P("walk", None, None), P("vec", "walk", None, None), P("vec", None), P("walk")),
        out_specs=(P("walk", None, None), P("walk", "vec", None), P("walk", None)),
        check_vma=False,
    )
```

```python
import functools

import jax
import jax.numpy as jnp
from jax import lax
from jax.experimental import pallas as pl
from jax.experimental.pallas import tpu as pltpu
from jax.sharding import PartitionSpec as P

MESH = pl.DeviceIdType.MESH
CHUNKS = 24
PARTS = 2
SKEW = 2
AHEAD = 3
QUEUE = (12, 14, 16, 18)
LEAF = ((3, 6, 9, 12), (6, 9, 12, 15), (12, 17), (17, 22))
HUB = ((16, 18, 20, 22), (19, 21, 23, 25), (24, 29), (29, 200))


def flip(index):
    return index + 1 - 2 * lax.rem(index, 2)


def walker_values(matrix, state):
    electrons = matrix.shape[0]
    orbitals = matrix.shape[1] // 2
    p = state[:orbitals, :]
    o = state[orbitals:, :]
    x = jnp.dot(matrix[:, :orbitals], p, preferred_element_type=jnp.float32)
    y = jnp.dot(matrix[:, orbitals:], p, preferred_element_type=jnp.float32)
    m_re = (x[:, :electrons] - y[:, electrons:]).astype(jnp.bfloat16)
    m_im = (x[:, electrons:] + y[:, :electrons]).astype(jnp.bfloat16)
    u = jnp.dot(m_re, o, preferred_element_type=jnp.float32)
    v = jnp.dot(m_im, o, preferred_element_type=jnp.float32)
    g_re = u[:, :electrons] - v[:, electrons:]
    g_im = u[:, electrons:] + v[:, :electrons]
    t_re, t_im = g_re.T, g_im.T
    eye = (lax.broadcasted_iota(jnp.int32, g_re.shape, 0)
           == lax.broadcasted_iota(jnp.int32, g_re.shape, 1))
    return [
        jnp.sum(jnp.where(eye, g_re, 0.0)),
        jnp.sum(jnp.where(eye, g_im, 0.0)),
        jnp.sum(g_re * t_re - g_im * t_im),
        2.0 * jnp.sum(g_re * t_im),
    ]


def step_kernel(
    n_walk, n_vec, flags, slots, chol, walkers, table, partner, branched,
    home, away, own, up, down, cand_0, cand_1, sel, matrix, state, result,
    bcast_send, home_sem, away_send, away_sem, relay_send,
    up_send, up_sem, down_send, down_sem,
    x_send, x_sem, z_send, z_sem, local_sem,
    y_send, y_sem, d_send, d_sem, r_send, r_sem,
    by_send, by_sem, bd_send, bd_sem, br_send, br_sem, self_sem,
    load_sem, t_send, t_sem,
):
    walk, vec = lax.axis_index("walk"), lax.axis_index("vec")
    rows = n_walk // 2
    row, col = walk // 2, lax.rem(walk, 2)
    low = lax.rem(vec, 2)
    hub = low == col
    cand = (cand_0, cand_1)
    chunks, depth = home.shape[0], home.shape[1]
    per_dev = walkers.shape[0]
    quarter = sel.shape[1]
    piece = quarter // PARTS
    pieces = [(w, t) for t in range(PARTS) for w in range(per_dev)]
    flip_walk, flip_vec = flip(walk), flip(vec)
    far_vec = lax.rem(vec + 2, n_vec)
    z_next = lax.rem(row + 1 - 2 * col + rows, rows)
    z_to = {"walk": z_next * 2 + col, "vec": vec}
    across = {"walk": flip_walk, "vec": vec}
    mate = {"walk": walk, "vec": flip_vec}
    over = {"walk": walk, "vec": far_vec}
    above = {"walk": walk + 2, "vec": vec}
    below = {"walk": walk - 2, "vec": vec}
    row_up, row_down = lax.rem(row + 1, rows), lax.rem(row + rows - 1, rows)

    place = col * n_vec + vec
    readers = [({"walk": walk, "vec": lax.rem(vec + j, n_vec)}, place) for j in range(1, n_vec)]
    readers += [({"walk": flip_walk, "vec": lax.rem(vec + j, n_vec)}, place) for j in range(n_vec)]
    readers += [({"walk": row_up * 2, "vec": lax.rem(vec + j, n_vec)}, place + 2 * n_vec) for j in range(n_vec)]
    readers += [({"walk": row_down * 2 + 1, "vec": lax.rem(vec + j, n_vec)}, place + 2 * n_vec) for j in range(n_vec)]

    bar = pltpu.get_barrier_semaphore()
    for target in (
        [t for t, _ in readers[:2 * n_vec - 1]]
        + [{"walk": r * 2 + c, "vec": lax.rem(vec + j, n_vec)}
           for r in (row_up, row_down) for c in range(2) for j in range(n_vec)]
    ):
        pl.semaphore_signal(bar, inc=1, device_id=target, device_id_type=MESH)
    pl.semaphore_wait(bar, 6 * n_vec - 1)

    def remote(src, dst, send, recv, target):
        return pltpu.make_async_remote_copy(
            src_ref=src, dst_ref=dst, send_sem=send, recv_sem=recv,
            device_id=target, device_id_type=MESH)

    def chol_rows(k):
        return chol.at[0, 0, pl.ds(pl.multiple_of(k * depth, depth), depth)]

    def own_to_home(k):
        return pltpu.make_async_copy(chol_rows(k), home.at[k], home_sem.at[k])

    def own_to_mate(k):
        return remote(chol_rows(k), home.at[k], bcast_send.at[k], home_sem.at[k], mate)

    def own_across(k):
        return remote(chol_rows(k), away.at[k], away_send.at[k], away_sem.at[k], across)

    def away_to_mate(k):
        return remote(away.at[k], away.at[k], relay_send.at[k], away_sem.at[k], mate)

    def send_up(k):
        return remote(up.at[k], up.at[k], up_send.at[k], up_sem.at[k], above)

    def send_down(k):
        return remote(down.at[k], down.at[k], down_send.at[k], down_sem.at[k], below)

    def part(index, t):
        return pl.ds(pl.multiple_of(index * quarter + t * piece, piece), piece)

    def inner(t):
        return pl.ds(t * piece, piece)

    far_base = col * 2 * per_dev
    near_base = (1 - col) * 2 * per_dev

    def walker_across(w, t):
        at = part(vec, t)
        return remote(walkers.at[w, at], partner.at[w, at], x_send.at[w, t], x_sem.at[w, t], across)

    def walker_z(w, t):
        return remote(partner.at[w, part(vec, t)], cand[t].at[far_base + w],
                      z_send.at[w, t], z_sem.at[w, t], z_to)

    def own_cand(w, t):
        return pltpu.make_async_copy(
            walkers.at[w, part(vec, t)], cand[t].at[per_dev + w], local_sem.at[w, t])

    def near_cand(w, t):
        return pltpu.make_async_copy(
            partner.at[w, part(vec, t)], cand[t].at[near_base + w], local_sem.at[w, PARTS + t])

    def walker_y(w, t):
        at = part(vec, t)
        return remote(partner.at[w, at], partner.at[w, at], y_send.at[w, t], y_sem.at[w, t], over)

    def walker_mate(w, t):
        at = part(vec, t)
        return remote(partner.at[w, at], partner.at[w, at], d_send.at[w, t], d_sem.at[w, t], mate)

    def walker_relay(w, t):
        at = part(far_vec, t)
        return remote(partner.at[w, at], partner.at[w, at], r_send.at[w, t], r_sem.at[w, t], mate)

    def slot_y(s, t):
        return remote(sel.at[s, inner(t)], branched.at[s, part(vec, t)], by_send.at[s, t], by_sem.at[s, t], over)

    def slot_mate(s, t):
        return remote(sel.at[s, inner(t)], branched.at[s, part(vec, t)], bd_send.at[s, t], bd_sem.at[s, t], mate)

    def slot_relay(s, t):
        at = part(far_vec, t)
        return remote(branched.at[s, at], branched.at[s, at], br_send.at[s, t], br_sem.at[s, t], mate)

    def slot_self(s, t):
        return pltpu.make_async_copy(sel.at[s, inner(t)], branched.at[s, part(vec, t)], self_sem.at[s, t])

    def each(lo, hi, f):
        def body(k, carry):
            f(k)
            return carry
        lax.fori_loop(lo, hi, body, 0)

    for w, t in pieces:
        own_cand(w, t).start()

    @pl.when(hub)
    def _():
        def start(k):
            own_to_home(k).start()

            @pl.when(k < AHEAD)
            def _():
                own_to_mate(k).start()

        for w, t in pieces:
            walker_across(w, t).start()
        each(0, chunks, start)

    @pl.when(jnp.logical_not(hub))
    def _():
        at = 0
        for n, (w, t) in enumerate(pieces):
            cut = min(QUEUE[min(n, len(QUEUE) - 1)], chunks)
            each(at, cut, lambda k: own_across(k).start())
            walker_across(w, t).start()
            at = cut
        each(at, chunks, lambda k: own_across(k).start())

    for w in range(per_dev):
        pltpu.make_async_copy(walkers.at[w], state.at[w], load_sem.at[w]).start()

    last = rows - 1
    here = flags[0] == 1
    below_or_here = flags[1] == 1
    from_home = flags[2] == 1

    def step(i):
        @pl.when(i < chunks)
        def _():
            @pl.when(hub)
            def _():
                own_across(i).wait_recv()
                away_to_mate(i).start()

                @pl.when(i + AHEAD < chunks)
                def _():
                    own_to_mate(i + AHEAD).start()

                own_to_home(i).wait()

            @pl.when(jnp.logical_not(hub))
            def _():
                own_to_mate(i).wait_recv()
                away_to_mate(i).wait_recv()

            own[i] = jnp.where(from_home, home[i], away[i])

        ku = i - SKEW * row
        kd = i - SKEW * (last - row)

        @pl.when(jnp.logical_and(ku >= 0, ku < chunks))
        def _():
            @pl.when(row == 0)
            def _():
                up[ku] = own[ku]

            @pl.when(row > 0)
            def _():
                send_up(ku).wait_recv()
                up[ku] = jnp.where(here, own[ku], up[ku])

            @pl.when(row < last)
            def _():
                send_up(ku).start()

        @pl.when(jnp.logical_and(kd >= 0, kd < chunks))
        def _():
            @pl.when(row == last)
            def _():
                down[kd] = own[kd]

            @pl.when(row < last)
            def _():
                send_down(kd).wait_recv()
                down[kd] = jnp.where(here, own[kd], down[kd])

            @pl.when(row > 0)
            def _():
                send_down(kd).start()

    def arrive(w, t):
        walker_across(w, t).wait_recv()
        walker_z(w, t).start()
        walker_y(w, t).start()
        walker_mate(w, t).start()
        near_cand(w, t).start()

    lines = 16

    def select(t):
        for w in range(per_dev):
            own_cand(w, t).wait()
            near_cand(w, t).wait()
            walker_z(w, t).wait_recv()
        for s in range(per_dev):
            index = slots[s]

            def pick(n, s=s, index=index):
                at = pl.ds(pl.multiple_of(t * piece + n * lines, lines), lines)
                sel[s, at, :] = cand[t][index, pl.ds(pl.multiple_of(n * lines, lines), lines), :]

            each(0, piece // lines, pick)
            slot_y(s, t).start()
            slot_mate(s, t).start()
            slot_self(s, t).start()

    def pass_on(w, t):
        walker_y(w, t).wait_recv()
        walker_relay(w, t).start()

    def pass_slots(t):
        for s in range(per_dev):
            slot_y(s, t).wait_recv()
            slot_relay(s, t).start()

    events = []
    for times, role in ((LEAF, jnp.logical_not(hub)), (HUB, hub)):
        for n, (w, t) in enumerate(pieces):
            n = min(n, len(times[0]) - 1)
            events.append((times[0][n], role, functools.partial(arrive, w, t)))
            events.append((times[1][n], role, functools.partial(pass_on, w, t)))
        for t in range(PARTS):
            events.append((times[2][t], role, functools.partial(select, t)))
            events.append((times[3][t], role, functools.partial(pass_slots, t)))
    events.sort(key=lambda event: event[0])

    def run(event):
        @pl.when(event[1])
        def _():
            event[2]()

    total = chunks + SKEW * last
    at = 0
    for event in events:
        if event[0] < 200:
            cut = min(event[0], total)
            if cut > at:
                each(at, cut, step)
                at = cut
            run(event)
    each(at, total, step)

    def finish(k):
        matrix[pl.ds(pl.multiple_of(k * depth, depth), depth), :] = jnp.where(below_or_here, up[k], down[k])

    each(0, chunks, finish)

    for w, t in pieces:
        walker_mate(w, t).wait_recv()
        walker_relay(w, t).wait_recv()

    def load(i):
        return pltpu.make_async_copy(partner.at[i], state.at[i], load_sem.at[i])

    sub = lax.broadcasted_iota(jnp.int32, result.shape, 0)
    lane = lax.broadcasted_iota(jnp.int32, result.shape, 1)
    result[...] = jnp.zeros_like(result)

    def compute(i):
        slot = lax.rem(i, per_dev)
        load(slot).wait()
        for n, value in enumerate(walker_values(matrix, state.at[slot])):
            result[...] = jnp.where(jnp.logical_and(sub == i, lane == n), value, result[...])

        @pl.when(i < per_dev)
        def _():
            load(slot).start()

    each(0, 2 * per_dev, compute)

    def tell(n):
        target, where = readers[n]
        return remote(result, table.at[where], t_send.at[n], t_sem.at[where], target)

    for n in range(len(readers)):
        tell(n).start()

    for event in events:
        if event[0] >= 200:
            run(event)

    table[place] = result[...]

    @pl.when(hub)
    def _():
        def ended(k):
            own_to_mate(k).wait_send()
            away_to_mate(k).wait_send()
        each(0, chunks, ended)

    @pl.when(jnp.logical_not(hub))
    def _():
        each(0, chunks, lambda k: own_across(k).wait_send())

    @pl.when(row < last)
    def _():
        each(0, chunks, lambda k: send_up(k).wait_send())

    @pl.when(row > 0)
    def _():
        each(0, chunks, lambda k: send_down(k).wait_send())

    for w, t in pieces:
        walker_across(w, t).wait_send()
        walker_z(w, t).wait_send()
        walker_y(w, t).wait_send()
        walker_mate(w, t).wait_send()
        walker_relay(w, t).wait_send()
    for n in range(len(readers)):
        tell(n).wait_send()

    for j in range(1, n_vec):
        v = lax.rem(vec + j, n_vec)
        remote(result, table.at[0], t_send.at[0], t_sem.at[col * n_vec + v], mate).wait_recv()
    for j in range(n_vec):
        remote(result, table.at[0], t_send.at[0], t_sem.at[(1 - col) * n_vec + j], mate).wait_recv()
    for j in range(2 * n_vec):
        remote(result, table.at[0], t_send.at[0], t_sem.at[2 * n_vec + j], mate).wait_recv()

    for t in range(PARTS):
        for s in range(per_dev):
            slot_y(s, t).wait_send()
            slot_mate(s, t).wait()
            slot_relay(s, t).wait()
            slot_self(s, t).wait()


def step_all(n_walk, n_vec, flags, slots, chol, walkers):
    per_dev, height, width = walkers.shape
    electrons, orbitals = chol.shape[2:]
    chunks = CHUNKS if electrons % (CHUNKS * 16) == 0 else 1
    depth = electrons // chunks
    big = pltpu.VMEM((chunks, depth, orbitals), chol.dtype)
    dma = pltpu.SemaphoreType.DMA
    any_spec = pl.BlockSpec(memory_space=pl.ANY)
    smem = pl.BlockSpec(memory_space=pltpu.SMEM)
    same = jax.ShapeDtypeStruct(walkers.shape, walkers.dtype)
    piece_sem = dma((per_dev, PARTS))
    return pl.pallas_call(
        functools.partial(step_kernel, n_walk, n_vec),
        out_shape=(jax.ShapeDtypeStruct((4 * n_vec, 8, 128), jnp.float32), same, same),
        in_specs=[smem, smem, any_spec, any_spec],
        out_specs=(pl.BlockSpec(memory_space=pltpu.VMEM), any_spec, any_spec),
        scratch_shapes=[
            big, big, big, big, big,
            pltpu.VMEM((3 * per_dev, height // n_vec // PARTS, width), walkers.dtype),
            pltpu.VMEM((3 * per_dev, height // n_vec // PARTS, width), walkers.dtype),
            pltpu.VMEM((per_dev, height // n_vec, width), walkers.dtype),
            pltpu.VMEM((electrons, orbitals), chol.dtype),
            pltpu.VMEM((per_dev, height, width), walkers.dtype),
            pltpu.VMEM((8, 128), jnp.float32),
        ] + [dma((chunks,))] * 9 + [piece_sem] * 4 + [dma((per_dev, 2 * PARTS))]
        + [piece_sem] * 13 + [dma((per_dev,)), dma((4 * n_vec - 1,)), dma((4 * n_vec,))],
        compiler_params=pltpu.CompilerParams(
            collective_id=0, has_side_effects=True, vmem_limit_bytes=60 * 1024 * 1024),
        name="step_all",
    )(flags, slots, chol, walkers)


def shards(n_walk, n_vec, walkers, chol, owners, branch_src):
    per_dev = walkers.shape[0]
    walk, vec = lax.axis_index("walk"), lax.axis_index("vec")
    row, col, low = walk // 2, walk % 2, vec % 2
    swap = [(i, i + 1 - 2 * (i % 2)) for i in range(n_vec)]
    mate_roots = lax.ppermute(owners[0], "vec", swap)
    roots = jnp.where(low == col, owners[0], mate_roots)
    root = jnp.take(roots, low)
    flags = jnp.stack([root // 2 == row, root // 2 <= row, root % 2 == col]).astype(jnp.int32)
    total = per_dev * n_walk
    relative = ((branch_src - (walk - 1) * per_dev + total) % total).astype(jnp.int32)
    table, _, branched = step_all(n_walk, n_vec, flags, relative, chol, walkers)
    table = table[:, :2 * per_dev, :4].reshape(2, 2, n_vec // 2, 2, 2, per_dev, 4)
    even, odd = table[:, 0], table[:, 1]
    first = jnp.stack([even[:, :, :, 0], odd[:, :, :, 1]], axis=2)
    second = jnp.stack([even[:, :, :, 1], odd[:, :, :, 0]], axis=2)
    both = jnp.stack([first, second], axis=1)
    both = jnp.transpose(both, (0, 1, 5, 2, 3, 4, 6)).reshape(4 * per_dev, n_vec, 2, 4)
    side = relative // per_dev
    block = jnp.where(side == 1, col, jnp.where(side == 2 * (1 - col), 1 - col, 3 - col))
    chosen = jnp.take(both, block * per_dev + relative % per_dev, axis=0)
    bias = lax.dynamic_slice_in_dim(chosen, vec, 1, axis=1)[:, 0, :, :2]
    energy = -0.5 * jnp.sum(chosen[..., 2:], axis=(1, 2))
    return (branched, bias, energy)


def solution(mesh):
    n_walk, n_vec = mesh.shape["walk"], mesh.shape["vec"]
    return jax.shard_map(
        functools.partial(shards, n_walk, n_vec),
        mesh=mesh,
        in_specs=(P("walk", None, None), P("vec", "walk", None, None), P("vec", None), P("walk")),
        out_specs=(P("walk", None, None), P("walk", "vec", None), P("walk", None)),
        check_vma=False,
    )
```
